512 devices in a mesh: heads: 8 (over x, core), frames: 64 (over z, y).
Axes of the slice: x: 4, y: 4, z: 16, core: 2. Of those that a mesh axis runs over, the one named last changes fastest.
Arguments:
- query_proj: bfloat16 [32768, 5120], P('frames', 'heads'), may hold values from -60 to 60
- key_proj: bfloat16 [32768, 5120], P('frames', 'heads'), may hold values from -60 to 60
- value_proj: bfloat16 [32768, 5120], P('frames', 'heads'), may hold values from -96 to 96
- query_gain: float32 [5120], P('heads'), may hold values from 0.1 to 1.9
- key_gain: float32 [5120], P('heads'), may hold values from 0.1 to 1.9
- key_blocks: int32 [64, 16], P('frames'), may hold values from 0 to 15, each once within a row
Outputs:
- attended: float32 [32768, 5120], P('frames', 'heads')
The draws below stay inside these ranges and needn't reach their ends.
Inputs may be any that keep to these rules, and one draw needn't show every extreme that they name: `key_blocks`: each row is a permutation of the key block numbers of one frame.
All inputs are finite; a program needn't handle non-finite values.
Results may differ from the reference program's by a relative error of at most 0.012.
Values may be sent and summed in bfloat16 or wider, within the bound.
No kernel may reach another device: no remote copies, remote signals or barrier semaphores. Data moves between devices by JAX's collectives and lax.ppermute only.
A program may use at most 64 MiB of HBM per device.

```python
import jax
import jax.numpy as jnp
from jax import lax

HD = 128
BS = 32
OCTAVES = 3
TOK_DEV = 512
HEADS = 40
TOKENS = 32768
N_FRAMES = 64


def projection_draw(key, salt):
    width_total = HEADS * HD
    sample = jax.random.normal(jax.random.fold_in(key, salt), (TOKENS, width_total), jnp.float32)
    column_ids = jnp.arange(width_total, dtype=jnp.float32)
    column_ramp = 1.0 + 2.0 * column_ids / (width_total - 1.0)
    sample = sample * column_ramp
    return jnp.clip(sample, -60.0, 60.0).astype(jnp.bfloat16)


def draw_query_proj(key, part):
    return projection_draw(key, 11)


def draw_key_proj(key, part):
    return projection_draw(key, 23)


def levels(own_key, dims, pieces, least, high):
    level, own = 1.0, jax.random.fold_in(own_key, 6)
    for dim, shards_of in pieces:
        steps = jnp.exp(jax.random.uniform(jax.random.fold_in(own, dim), (shards_of,), jnp.float32, least / len(pieces), high / len(pieces)))
        level = level * jnp.repeat(steps, dims[dim] // shards_of).reshape([-1 if axis == dim else 1 for axis in range(len(dims))])
    return level


def normal_values(key, extent, spread, reach, cuts=(), kind=jnp.bfloat16):
    values = jax.random.normal(key, extent, jnp.float32) * spread
    if len(cuts) > 0:
        values = levels(key, extent, cuts, -0.22, 0.18) * values
    return jnp.clip(values, min=-reach, max=reach).astype(kind)


def setup_inputs(seed: int = 0) -> dict:
    splits = jax.random.split(jax.random.key(seed), 7)
    return {
        "query_proj": draw_query_proj(jax.random.fold_in(splits[6], 71), 0),
        "key_proj": draw_key_proj(jax.random.fold_in(splits[6], 71), 0),
        "value_proj": normal_values(splits[2], (TOKENS, HEADS * HD), 16.0, 96.0, ((0, 64), (1, 8))),
        "query_gain": jnp.clip(1.0 + 0.18 * jax.random.normal(splits[3], (HEADS * HD,), jnp.float32), 0.1, 1.9),
        "key_gain": jnp.clip(1.0 + 0.18 * jax.random.normal(splits[4], (HEADS * HD,), jnp.float32), 0.1, 1.9),
        "key_blocks": jax.vmap(lambda own: jax.random.permutation(own, TOK_DEV // BS))(jax.random.split(splits[5], N_FRAMES)).reshape((N_FRAMES, TOK_DEV // BS)).astype(jnp.int32),
    }


EPS = 1e-06

def normed(inputs, gain_row):
    as_float = inputs.astype(jnp.float32)
    mean_sq = lax.optimization_barrier(jnp.mean(as_float * as_float, axis=1, keepdims=True))
    return (as_float * lax.rsqrt(mean_sq + EPS) * gain_row).astype(jnp.bfloat16)

def reference(query_proj, key_proj, value_proj, query_gain, key_gain, key_blocks):
    feature_width = query_proj.shape[1]
    head_count = feature_width // HD
    q_hat = normed(query_proj, query_gain)
    k_hat = normed(key_proj, key_gain)
    block_size = TOK_DEV // key_blocks.shape[1]
    row_order = (key_blocks[:, :, None] * block_size + jnp.arange(block_size, dtype=jnp.int32)).reshape(N_FRAMES, TOK_DEV).astype(jnp.int32)
    keys_frames = k_hat.reshape(N_FRAMES, TOK_DEV, feature_width)
    value_frames = value_proj.reshape(N_FRAMES, TOK_DEV, feature_width)
    query_frames = q_hat.reshape(N_FRAMES, TOK_DEV, feature_width)

    def one_frame(frame_index):
        key_parts = [keys_frames[frame_index]]
        value_parts = [value_frames[frame_index]]
        validity = [jnp.ones((TOK_DEV,), dtype=bool)]
        for octave in range(OCTAVES):
            kept_rows = TOK_DEV >> octave
            frame_span = 1 << octave
            for direction in (1, -1):
                partner_frames = frame_index + direction * (frame_span + jnp.arange(frame_span, dtype=jnp.int32))
                inside = (partner_frames >= 0) & (partner_frames < N_FRAMES)
                clipped = jnp.clip(partner_frames, 0, N_FRAMES - 1).astype(jnp.int32)
                picked_rows = row_order[clipped][:, :kept_rows]
                key_parts.append(keys_frames[clipped[:, None], picked_rows].reshape(frame_span * kept_rows, feature_width))
                value_parts.append(value_frames[clipped[:, None], picked_rows].reshape(frame_span * kept_rows, feature_width))
                validity.append(jnp.repeat(inside, kept_rows))
        all_keys = jnp.concatenate(key_parts, axis=0)
        all_values = jnp.concatenate(value_parts, axis=0)
        key_total = all_keys.shape[0]
        score_bias = jnp.where(jnp.concatenate(validity), 0.0, -1e+30).astype(jnp.float32)
        query_heads = query_frames[frame_index].reshape(TOK_DEV, head_count, HD).transpose(1, 0, 2)
        key_heads = all_keys.reshape(key_total, head_count, HD).transpose(1, 0, 2)
        value_heads = all_values.reshape(key_total, head_count, HD).transpose(1, 0, 2)

        def attend_head(triple):
            query_head, key_head, value_head = triple
            scores = jnp.dot(query_head.astype(jnp.float32), key_head.astype(jnp.float32).T, precision=lax.Precision.HIGHEST) * HD ** (-0.5) + score_bias
            row_max = lax.optimization_barrier(jnp.max(scores, axis=1, keepdims=True))
            weights = jnp.exp(scores - row_max)
            totals = lax.optimization_barrier(jnp.sum(weights, axis=1, keepdims=True))
            rounded = weights.astype(jnp.bfloat16)
            mixed = jnp.dot(rounded.astype(jnp.float32), value_head.astype(jnp.float32), precision=lax.Precision.HIGHEST)
            return mixed / totals
        result = lax.map(attend_head, (query_heads, key_heads, value_heads))
        return result.transpose(1, 0, 2).reshape(TOK_DEV, feature_width)
    frames_out = lax.map(one_frame, jnp.arange(N_FRAMES, dtype=jnp.int32))
    return frames_out.reshape(TOKENS, feature_width)
```

```python
import functools
import math

import jax
import jax.numpy as jnp
from jax import lax
from jax.experimental import pallas as pl
from jax.experimental.pallas import tpu as pltpu
from jax.sharding import PartitionSpec as P

HD = 128
EPS = 1e-06
LOG2E = math.log2(math.e)
VMEM_LIMIT = 48 << 20
FAR = 1e30


def shift(value, steps):
    count = lax.axis_size("frames")
    initial, last = (max(0, -steps), min(count, count - steps))
    return lax.ppermute(
        value, "frames", [(source, source + steps) for source in range(initial, last)]
    )


def row_squares(value):
    wide = value.astype(jnp.float32)
    wide = wide * wide
    folded = wide[:, :HD]
    for start in range(HD, value.shape[1], HD):
        folded = folded + wide[:, start : start + HD]
    return jnp.sum(folded.T, axis=0, keepdims=True)


def gather_kernel(blocks_ref, query_ref, key_ref, value_ref, ranked_ref, squares_ref):
    block_count = blocks_ref.shape[1]
    size = value_ref.shape[0] // block_count
    for rank in range(block_count):
        start = pl.multiple_of(blocks_ref[0, rank] * size, size)
        ranked_ref[rank * size : (rank + 1) * size, :] = value_ref[pl.ds(start, size), :]
    squares_ref[0:1, :] = row_squares(query_ref[...])
    squares_ref[1:2, :] = row_squares(key_ref[...])


def norm_kernel(
    width_total,
    blocks_ref,
    squares_ref,
    query_ref,
    key_ref,
    ranked_value_ref,
    query_gain_ref,
    key_gain_ref,
    query_out_ref,
    key_out_ref,
    half_ref,
    plain_ref,
):
    rows, width = query_ref.shape
    factors = lax.rsqrt(squares_ref[...] / width_total + EPS)
    query_factor = jnp.broadcast_to(factors[0:1, :], (HD, rows)).T
    key_factor = jnp.broadcast_to(factors[1:2, :], (HD, rows)).T
    for start in range(0, width, HD):
        lanes = slice(start, start + HD)
        query = query_ref[:, lanes].astype(jnp.float32)
        query_out_ref[:, lanes] = (query * query_factor * query_gain_ref[:, lanes]).astype(
            jnp.bfloat16
        )
        key = key_ref[:, lanes].astype(jnp.float32)
        plain_ref[:, lanes] = (key * key_factor * key_gain_ref[:, lanes]).astype(jnp.bfloat16)
    block_count = blocks_ref.shape[1]
    size = rows // block_count
    for rank in range(block_count):
        start = pl.multiple_of(blocks_ref[0, rank] * size, size)
        key_out_ref[rank * size : (rank + 1) * size, :] = plain_ref[pl.ds(start, size), :]
    half = rows // 2
    half_ref[:half, :] = key_out_ref[:half, :]
    half_ref[half:, :] = ranked_value_ref[:half, :]


def attend_kernel(pieces, first, last, operand_count, valid_ref, query_ref, *refs):
    operands = refs[:operand_count]
    rest = refs[operand_count:]
    if not first:
        old_mixed_ref, old_stats_ref = rest[:2]
        rest = rest[2:]
    rows, width = query_ref.shape
    scale = HD ** (-0.5) * LOG2E
    for head in range(width // HD):
        lanes = slice(head * HD, (head + 1) * HD)
        query = query_ref[:, lanes]
        tops = []
        scores = []
        for key_at, key_start, _, _, count, flag in pieces:
            key = operands[key_at][key_start : key_start + count, lanes]
            score = lax.dot_general(
                key, query, (((1,), (1,)), ((), ())), preferred_element_type=jnp.float32
            )
            top = jnp.max(score, axis=0, keepdims=True) * scale
            if flag is not None:
                top = jnp.where(valid_ref[flag] > 0, top, -FAR)
            scores.append(score)
            tops.append(top)
        top = functools.reduce(jnp.maximum, tops)
        if not first:
            old_top = old_stats_ref[head : head + 1, :]
            top = jnp.maximum(top, old_top)
            keep = jnp.exp2(old_top - top)
        total = None
        weights = []
        values = []
        for score, (_, _, value_at, value_start, count, flag) in zip(scores, pieces):
            level = top if flag is None else jnp.where(valid_ref[flag] > 0, top, FAR)
            weight = jnp.exp2(score * scale - level)
            part = jnp.sum(weight, axis=0, keepdims=True)
            total = part if total is None else total + part
            weights.append(weight.astype(jnp.bfloat16))
            values.append(operands[value_at][value_start : value_start + count, lanes])
        weights = weights[0] if len(weights) == 1 else jnp.concatenate(weights, axis=0)
        values = values[0] if len(values) == 1 else jnp.concatenate(values, axis=0)
        mixed = lax.dot_general(
            values, weights, (((0,), (0,)), ((), ())), preferred_element_type=jnp.float32
        )
        if not first:
            mixed = mixed + keep * old_mixed_ref[head * HD : (head + 1) * HD, :]
            total = total + keep * old_stats_ref[8 + head : 9 + head, :]
        if last:
            rest[0][:, lanes] = (mixed / total).T
        else:
            rest[0][head * HD : (head + 1) * HD, :] = mixed
            rest[1][head : head + 1, :] = top
            rest[1][8 + head : 9 + head, :] = total


def attend(query, operands, pieces, valid, state=None, last=False):
    rows, width = query.shape
    heads = width // HD
    keys = sum(piece[4] for piece in pieces)
    first = state is None
    mixed = jax.ShapeDtypeStruct((width, rows), jnp.float32)
    stats = jax.ShapeDtypeStruct((16, rows), jnp.float32)
    out = jax.ShapeDtypeStruct((rows, width), jnp.float32)
    inputs = [valid, query, *operands] + ([] if first else list(state))
    vmem = pl.BlockSpec(memory_space=pltpu.VMEM)
    aliases = {}
    if not first and not last:
        aliases = {len(inputs) - 2: 0, len(inputs) - 1: 1}
    moved = 2 * (query.size + sum(operand.size for operand in operands)) + 8 * rows * width
    return pl.pallas_call(
        functools.partial(attend_kernel, pieces, first, last, len(operands)),
        out_shape=out if last else (mixed, stats),
        in_specs=[pl.BlockSpec(memory_space=pltpu.SMEM)] + [vmem] * (len(inputs) - 1),
        out_specs=vmem if last else (vmem, vmem),
        input_output_aliases=aliases,
        compiler_params=pltpu.CompilerParams(vmem_limit_bytes=VMEM_LIMIT),
        cost_estimate=pl.CostEstimate(
            flops=4 * rows * keys * width,
            bytes_accessed=moved,
            transcendentals=rows * keys * heads,
        ),
    )(*inputs)


def on_device(query_proj, key_proj, value_proj, query_gain, key_gain, key_blocks):
    rows, width = query_proj.shape
    width_total = width * lax.axis_size("heads")
    frame_count = lax.axis_size("frames")
    frame = lax.axis_index("frames")
    half, quarter = rows // 2, rows // 4
    smem = pl.BlockSpec(memory_space=pltpu.SMEM)
    vmem = pl.BlockSpec(memory_space=pltpu.VMEM)
    params = pltpu.CompilerParams(vmem_limit_bytes=VMEM_LIMIT)
    block = jax.ShapeDtypeStruct((rows, width), jnp.bfloat16)

    own_value, squares = pl.pallas_call(
        gather_kernel,
        out_shape=(block, jax.ShapeDtypeStruct((2, rows), jnp.float32)),
        in_specs=[smem, vmem, vmem, vmem],
        out_specs=(vmem, vmem),
        compiler_params=params,
        cost_estimate=pl.CostEstimate(flops=4 * rows * width, bytes_accessed=8 * rows * width, transcendentals=0),
    )(key_blocks, query_proj, key_proj, value_proj)
    near_value = [shift(own_value, step) for step in (1, -1)]
    squares = lax.psum(squares, "heads")
    query, own_key, own_half = pl.pallas_call(
        functools.partial(norm_kernel, width_total),
        out_shape=(block, block, block),
        in_specs=[smem] + [vmem] * 6,
        out_specs=(vmem, vmem, vmem),
        scratch_shapes=[pltpu.VMEM((rows, width), jnp.bfloat16)],
        compiler_params=params,
        cost_estimate=pl.CostEstimate(flops=6 * rows * width, bytes_accessed=12 * rows * width, transcendentals=0),
    )(
        key_blocks,
        squares,
        query_proj,
        key_proj,
        own_value,
        query_gain.reshape(1, width),
        key_gain.reshape(1, width),
    )
    near_key = [shift(own_key, step) for step in (1, -1)]
    third = [shift(own_half, 3 * step) for step in (1, -1)]
    relayed = [jnp.concatenate([key[:half], value[:half]]) for key, value in zip(near_key, near_value)]
    second = [shift(value, step) for value, step in zip(relayed, (1, -1))]
    far = [
        shift(
            jnp.concatenate(
                [
                    own_key[:quarter],
                    near_key[side][:quarter],
                    third[side][:quarter],
                    own_value[:quarter],
                    near_value[side][:quarter],
                    third[side][half : half + quarter],
                ]
            ),
            4 * step,
        )
        for side, step in enumerate((1, -1))
    ]
    sixth = [
        shift(jnp.concatenate([second[side][:quarter], second[side][half : half + quarter]]), 4 * step)
        for side, step in enumerate((1, -1))
    ]

    distance = jnp.arange(1, 8, dtype=jnp.int32)
    valid = jnp.concatenate([frame - distance >= 0, frame + distance < frame_count]).astype(jnp.int32)

    def flag(side, steps):
        return side * 7 + steps - 1

    state = attend(query, [own_key, own_value], [(0, 0, 1, 0, rows, None)], valid)
    state = attend(
        query,
        [*near_key, *near_value],
        [(side, 0, 2 + side, 0, rows, flag(side, 1)) for side in range(2)],
        valid,
        state,
    )
    state = attend(
        query, third, [(side, 0, side, half, half, flag(side, 3)) for side in range(2)], valid, state
    )
    state = attend(
        query, second, [(side, 0, side, half, half, flag(side, 2)) for side in range(2)], valid, state
    )
    state = attend(
        query,
        far,
        [
            (side, place * quarter, side, (3 + place) * quarter, quarter, flag(side, steps))
            for side in range(2)
            for place, steps in enumerate((4, 5, 7))
        ],
        valid,
        state,
    )
    return attend(
        query,
        sixth,
        [(side, 0, side, quarter, quarter, flag(side, 6)) for side in range(2)],
        valid,
        state,
        last=True,
    )


def solution(mesh):
    placed = (
        P("frames", "heads"),
        P("frames", "heads"),
        P("frames", "heads"),
        P("heads"),
        P("heads"),
        P("frames", None),
    )
    return jax.shard_map(
        on_device, mesh=mesh, in_specs=placed, out_specs=P("frames", "heads"), check_vma=False
    )
```

```python
import functools
import math

import jax
import jax.numpy as jnp
from jax import lax
from jax.experimental import pallas as pl
from jax.experimental.pallas import tpu as pltpu
from jax.sharding import PartitionSpec as P

HD = 128
EPS = 1e-06
LOG2E = math.log2(math.e)
VMEM_LIMIT = 20 << 20
FAR = 1e30


def shift(value, steps):
    count = lax.axis_size("frames")
    initial, last = (max(0, -steps), min(count, count - steps))
    return lax.ppermute(
        value, "frames", [(source, source + steps) for source in range(initial, last)]
    )


def row_squares(value):
    wide = value.astype(jnp.float32)
    wide = wide * wide
    folded = wide[:, :HD]
    for start in range(HD, value.shape[1], HD):
        folded = folded + wide[:, start : start + HD]
    return jnp.sum(folded.T, axis=0, keepdims=True)


def gather_kernel(
    blocks_ref, query_hbm, key_hbm, value_hbm, ranked_ref, squares_ref, query_ref, key_ref, value_ref, sems
):
    copies = [
        pltpu.make_async_copy(source, target, sems.at[place])
        for place, (source, target) in enumerate(
            ((value_hbm, value_ref), (query_hbm, query_ref), (key_hbm, key_ref))
        )
    ]
    for copy in copies:
        copy.start()
    copies[0].wait()
    block_count = blocks_ref.shape[1]
    size = value_ref.shape[0] // block_count
    for rank in range(block_count):
        start = pl.multiple_of(blocks_ref[0, rank] * size, size)
        ranked_ref[rank * size : (rank + 1) * size, :] = value_ref[pl.ds(start, size), :]
    copies[1].wait()
    query_squares = row_squares(query_ref[...])
    copies[2].wait()
    key_squares = row_squares(key_ref[...])
    for device in range(squares_ref.shape[0]):
        squares_ref[device, 0:1, :] = query_squares
        squares_ref[device, 1:2, :] = key_squares


def norm_kernel(
    width_total,
    blocks_ref,
    squares_ref,
    query_gain_ref,
    key_gain_ref,
    ranked_value_ref,
    query_hbm,
    key_hbm,
    query_out_ref,
    key_out_ref,
    half_ref,
    quarter_ref,
    query_ref,
    key_ref,
    sems,
):
    copies = [
        pltpu.make_async_copy(source, target, sems.at[place])
        for place, (source, target) in enumerate(((key_hbm, key_ref), (query_hbm, query_ref)))
    ]
    for copy in copies:
        copy.start()
    rows, width = query_ref.shape
    squares = squares_ref[0]
    for device in range(1, squares_ref.shape[0]):
        squares = squares + squares_ref[device]
    factors = lax.rsqrt(squares / width_total + EPS)
    query_factor = jnp.broadcast_to(factors[0:1, :], (HD, rows)).T
    key_factor = jnp.broadcast_to(factors[1:2, :], (HD, rows)).T
    copies[0].wait()
    for start in range(0, width, HD):
        lanes = slice(start, start + HD)
        key = key_ref[:, lanes].astype(jnp.float32)
        key_ref[:, lanes] = (key * key_factor * key_gain_ref[:, lanes]).astype(jnp.bfloat16)
    block_count = blocks_ref.shape[1]
    size = rows // block_count
    half, quarter = rows // 2, rows // 4
    for rank in range(block_count):
        start = pl.multiple_of(blocks_ref[0, rank] * size, size)
        block = key_ref[pl.ds(start, size), :]
        at = rank * size
        key_out_ref[at : at + size, :] = block
        if at < half:
            half_ref[at : at + size, :] = block
        if at < quarter:
            quarter_ref[at : at + size, :] = block
    half_ref[half:, :] = ranked_value_ref[:half, :]
    quarter_ref[quarter:, :] = ranked_value_ref[:quarter, :]
    copies[1].wait()
    for start in range(0, width, HD):
        lanes = slice(start, start + HD)
        query = query_ref[:, lanes].astype(jnp.float32)
        query_out_ref[:, lanes] = (query * query_factor * query_gain_ref[:, lanes]).astype(
            jnp.bfloat16
        )


def pack_kernel(parts, *refs):
    sources, (target_ref, sems) = refs[:-2], refs[-2:]
    copies = []
    at = 0
    for place, (source, start, count) in enumerate(parts):
        copies.append(
            pltpu.make_async_copy(
                sources[source].at[pl.ds(start, count), :],
                target_ref.at[pl.ds(at, count), :],
                sems.at[place],
            )
        )
        at += count
    for copy in copies:
        copy.start()
    for copy in copies:
        copy.wait()


def pack(sources, parts):
    width = sources[0].shape[1]
    rows = sum(count for _, _, count in parts)
    anywhere = pl.BlockSpec(memory_space=pl.ANY)
    return pl.pallas_call(
        functools.partial(pack_kernel, parts),
        out_shape=jax.ShapeDtypeStruct((rows, width), jnp.bfloat16),
        in_specs=[anywhere] * len(sources),
        out_specs=anywhere,
        scratch_shapes=[pltpu.SemaphoreType.DMA((len(parts),))],
        compiler_params=pltpu.CompilerParams(vmem_limit_bytes=1 << 20),
        cost_estimate=pl.CostEstimate(flops=0, bytes_accessed=4 * rows * width, transcendentals=0),
    )(*sources)


def attend_kernel(pieces, first, last, operand_count, valid_ref, query_ref, *refs):
    operands = refs[:operand_count]
    rest = refs[operand_count:]
    if not first:
        old_mixed_ref, old_stats_ref = rest[:2]
        rest = rest[2:]
    rows, width = query_ref.shape
    heads = width // HD
    scale = HD ** (-0.5) * LOG2E

    def lanes_of(head):
        return slice(head * HD, (head + 1) * HD)

    def score(head):
        query = query_ref[:, lanes_of(head)]
        return [
            lax.dot_general(
                operands[key_at][start : start + count, lanes_of(head)],
                query,
                (((1,), (1,)), ((), ())),
                preferred_element_type=jnp.float32,
            )
            for key_at, start, _, _, count, _ in pieces
        ]

    def weigh(head, scores):
        tops = []
        for part, (*_, flag) in zip(scores, pieces):
            top = jnp.max(part, axis=0, keepdims=True) * scale
            tops.append(top if flag is None else jnp.where(valid_ref[flag] > 0, top, -FAR))
        top = functools.reduce(jnp.maximum, tops)
        keep = None
        if not first:
            old_top = old_stats_ref[head : head + 1, :]
            top = jnp.maximum(top, old_top)
            keep = jnp.exp2(old_top - top)
        total = None
        weights = []
        for part, (*_, flag) in zip(scores, pieces):
            level = top if flag is None else jnp.where(valid_ref[flag] > 0, top, FAR)
            weight = jnp.exp2(part * scale - level)
            added = jnp.sum(weight, axis=0, keepdims=True)
            total = added if total is None else total + added
            weights.append(weight.astype(jnp.bfloat16))
        weights = weights[0] if len(weights) == 1 else jnp.concatenate(weights, axis=0)
        return top, keep, total, weights

    def mix(head, top, keep, total, weights):
        values = [
            operands[value_at][start : start + count, lanes_of(head)]
            for _, _, value_at, start, count, _ in pieces
        ]
        values = values[0] if len(values) == 1 else jnp.concatenate(values, axis=0)
        mixed = lax.dot_general(
            values, weights, (((0,), (0,)), ((), ())), preferred_element_type=jnp.float32
        )
        if not first:
            mixed = mixed + keep * old_mixed_ref[lanes_of(head), :]
            total = total + keep * old_stats_ref[8 + head : 9 + head, :]
        if last:
            rest[0][:, lanes_of(head)] = (mixed / total).T
        else:
            rest[0][lanes_of(head), :] = mixed
            rest[1][head : head + 1, :] = top
            rest[1][8 + head : 9 + head, :] = total

    scores = score(0)
    waiting = None
    for head in range(heads):
        following = score(head + 1) if head + 1 < heads else None
        weighed = weigh(head, scores)
        if waiting is not None:
            mix(*waiting)
        waiting = (head, *weighed)
        scores = following
    mix(*waiting)


def attend(query, operands, pieces, valid, state=None, last=False):
    rows, width = query.shape
    heads = width // HD
    keys = sum(piece[4] for piece in pieces)
    first = state is None
    mixed = jax.ShapeDtypeStruct((width, rows), jnp.float32)
    stats = jax.ShapeDtypeStruct((16, rows), jnp.float32)
    out = jax.ShapeDtypeStruct((rows, width), jnp.float32)
    inputs = [valid, query, *operands] + ([] if first else list(state))
    vmem = pl.BlockSpec(memory_space=pltpu.VMEM)
    aliases = {}
    if not first and not last:
        aliases = {len(inputs) - 2: 0, len(inputs) - 1: 1}
    moved = 2 * (query.size + sum(operand.size for operand in operands)) + 8 * rows * width
    return pl.pallas_call(
        functools.partial(attend_kernel, pieces, first, last, len(operands)),
        out_shape=out if last else (mixed, stats),
        in_specs=[pl.BlockSpec(memory_space=pltpu.SMEM)] + [vmem] * (len(inputs) - 1),
        out_specs=vmem if last else (vmem, vmem),
        input_output_aliases=aliases,
        compiler_params=pltpu.CompilerParams(vmem_limit_bytes=VMEM_LIMIT),
        cost_estimate=pl.CostEstimate(
            flops=4 * rows * keys * width,
            bytes_accessed=moved,
            transcendentals=rows * keys * heads,
        ),
    )(*inputs)


def on_device(query_proj, key_proj, value_proj, query_gain, key_gain, key_blocks):
    rows, width = query_proj.shape
    width_total = width * lax.axis_size("heads")
    frame_count = lax.axis_size("frames")
    frame = lax.axis_index("frames")
    half, quarter = rows // 2, rows // 4
    smem = pl.BlockSpec(memory_space=pltpu.SMEM)
    vmem = pl.BlockSpec(memory_space=pltpu.VMEM)
    params = pltpu.CompilerParams(vmem_limit_bytes=VMEM_LIMIT)
    block = jax.ShapeDtypeStruct((rows, width), jnp.bfloat16)

    anywhere = pl.BlockSpec(memory_space=pltpu.HBM)
    devices = lax.axis_size("heads")
    own_value, squares = pl.pallas_call(
        gather_kernel,
        out_shape=(block, jax.ShapeDtypeStruct((devices, 2, rows), jnp.float32)),
        in_specs=[smem, anywhere, anywhere, anywhere],
        out_specs=(vmem, vmem),
        scratch_shapes=[pltpu.VMEM((rows, width), jnp.bfloat16)] * 3 + [pltpu.SemaphoreType.DMA((3,))],
        compiler_params=params,
        cost_estimate=pl.CostEstimate(flops=4 * rows * width, bytes_accessed=8 * rows * width, transcendentals=0),
    )(key_blocks, *(pltpu.with_memory_space_constraint(x, pltpu.HBM) for x in (query_proj, key_proj, value_proj)))
    near_value = [shift(own_value, step) for step in (1, -1)]
    squares = lax.all_to_all(squares, "heads", 0, 0)
    part = lambda count: jax.ShapeDtypeStruct((count, width), jnp.bfloat16)
    query, own_key, own_half, own_quarter = pl.pallas_call(
        functools.partial(norm_kernel, width_total),
        out_shape=(block, block, block, part(half)),
        in_specs=[smem] + [vmem] * 4 + [anywhere] * 2,
        out_specs=(vmem,) * 4,
        scratch_shapes=[pltpu.VMEM((rows, width), jnp.bfloat16)] * 2 + [pltpu.SemaphoreType.DMA((2,))],
        compiler_params=params,
        cost_estimate=pl.CostEstimate(flops=6 * rows * width, bytes_accessed=12 * rows * width, transcendentals=0),
    )(
        key_blocks,
        squares,
        query_gain.reshape(1, width),
        key_gain.reshape(1, width),
        own_value,
        query_proj,
        key_proj,
    )
    distance = jnp.arange(1, 8, dtype=jnp.int32)
    valid = jnp.concatenate([frame - distance >= 0, frame + distance < frame_count]).astype(jnp.int32)

    def flag(side, steps):
        return side * 7 + steps - 1

    both = (1, -1)
    sides = (0, 1)
    near_key = [shift(own_key, step) for step in both]
    state = attend(query, [own_key, own_value], [(0, 0, 1, 0, rows, None)], valid)
    own_half, own_quarter, near_value, state = lax.optimization_barrier(
        (own_half, own_quarter, near_value, state)
    )
    third = [shift(own_half, 3 * step) for step in both]
    fourth = [shift(own_quarter, 4 * step) for step in both]
    *near_key, state = lax.optimization_barrier((*near_key, state))
    relayed = [pack([near_key[side], near_value[side]], [(0, 0, half), (1, 0, half)]) for side in sides]
    second = [shift(value, step) for value, step in zip(relayed, both)]
    passed = [
        pack(
            [near_key[side], near_value[side], third[side]],
            [(0, 0, quarter), (2, 0, quarter), (1, 0, quarter), (2, half, quarter)],
        )
        for side in sides
    ]
    far = [shift(value, 4 * step) for value, step in zip(passed, both)]
    near_key = list(lax.optimization_barrier((*near_key, *relayed, *passed))[:2])
    state = attend(
        query,
        [*near_key, *near_value],
        [(side, 0, 2 + side, 0, rows, flag(side, 1)) for side in sides],
        valid,
        state,
    )
    state = attend(
        query,
        [*third, *fourth],
        [(side, 0, side, half, half, flag(side, 3)) for side in sides]
        + [(2 + side, 0, 2 + side, quarter, quarter, flag(side, 4)) for side in sides],
        valid,
        state,
    )
    *second, state = lax.optimization_barrier((*second, state))
    sixth = [
        shift(pack([second[side]], [(0, 0, quarter), (0, half, quarter)]), 4 * step)
        for side, step in enumerate(both)
    ]
    state = attend(
        query,
        second,
        [(side, 0, side, half, half, flag(side, 2)) for side in sides],
        valid,
        state,
    )
    state = attend(
        query,
        far,
        [
            (side, place * quarter, side, (2 + place) * quarter, quarter, flag(side, steps))
            for side in sides
            for place, steps in enumerate((5, 7))
        ],
        valid,
        state,
    )
    return attend(
        query,
        sixth,
        [(side, 0, side, quarter, quarter, flag(side, 6)) for side in sides],
        valid,
        state,
        last=True,
    )


def solution(mesh):
    placed = (
        P("frames", "heads"),
        P("frames", "heads"),
        P("frames", "heads"),
        P("heads"),
        P("heads"),
        P("frames", None),
    )
    return jax.shard_map(
        on_device, mesh=mesh, in_specs=placed, out_specs=P("frames", "heads"), check_vma=False
    )
```

```python
import functools
import math

import jax
import jax.numpy as jnp
from jax import lax
from jax.experimental import pallas as pl
from jax.experimental.pallas import tpu as pltpu
from jax.sharding import PartitionSpec as P

HD = 128
EPS = 1e-06
LOG2E = math.log2(math.e)
VMEM_LIMIT = 20 << 20
FAR = 1e30


def shift(value, steps):
    count = lax.axis_size("frames")
    initial, last = (max(0, -steps), min(count, count - steps))
    return lax.ppermute(
        value, "frames", [(source, source + steps) for source in range(initial, last)]
    )


def row_squares(value):
    wide = value.astype(jnp.float32)
    wide = wide * wide
    folded = wide[:, :HD]
    for start in range(HD, value.shape[1], HD):
        folded = folded + wide[:, start : start + HD]
    return jnp.sum(folded.T, axis=0, keepdims=True)


def gather_kernel(
    blocks_hbm,
    query_hbm,
    key_hbm,
    value_hbm,
    ranked_ref,
    squares_ref,
    blocks_ref,
    query_ref,
    key_ref,
    value_ref,
    sems,
):
    copies = [
        pltpu.make_async_copy(source, target, sems.at[place])
        for place, (source, target) in enumerate(
            (
                (value_hbm, value_ref),
                (query_hbm, query_ref),
                (key_hbm, key_ref),
                (blocks_hbm, blocks_ref),
            )
        )
    ]
    for copy in copies:
        copy.start()
    copies[3].wait()
    copies[0].wait()
    block_count = blocks_ref.shape[1]
    size = value_ref.shape[0] // block_count
    for rank in range(block_count):
        start = pl.multiple_of(blocks_ref[0, rank] * size, size)
        ranked_ref[rank * size : (rank + 1) * size, :] = value_ref[pl.ds(start, size), :]
    copies[1].wait()
    query_squares = row_squares(query_ref[...])
    copies[2].wait()
    key_squares = row_squares(key_ref[...])
    for device in range(squares_ref.shape[0]):
        squares_ref[device, 0:1, :] = query_squares
        squares_ref[device, 1:2, :] = key_squares


def norm_kernel(
    width_total,
    blocks_ref,
    squares_ref,
    query_gain_ref,
    key_gain_ref,
    ranked_value_ref,
    query_hbm,
    key_hbm,
    query_out_ref,
    key_out_ref,
    half_ref,
    quarter_ref,
    query_ref,
    key_ref,
    sems,
):
    copies = [
        pltpu.make_async_copy(source, target, sems.at[place])
        for place, (source, target) in enumerate(((key_hbm, key_ref), (query_hbm, query_ref)))
    ]
    for copy in copies:
        copy.start()
    rows, width = query_ref.shape
    squares = squares_ref[0]
    for device in range(1, squares_ref.shape[0]):
        squares = squares + squares_ref[device]
    factors = lax.rsqrt(squares / width_total + EPS)
    query_factor = jnp.broadcast_to(factors[0:1, :], (HD, rows)).T
    key_factor = jnp.broadcast_to(factors[1:2, :], (HD, rows)).T
    copies[0].wait()
    for start in range(0, width, HD):
        lanes = slice(start, start + HD)
        key = key_ref[:, lanes].astype(jnp.float32)
        key_ref[:, lanes] = (key * key_factor * key_gain_ref[:, lanes]).astype(jnp.bfloat16)
    block_count = blocks_ref.shape[1]
    size = rows // block_count
    half, quarter = rows // 2, rows // 4
    for rank in range(block_count):
        start = pl.multiple_of(blocks_ref[0, rank] * size, size)
        block = key_ref[pl.ds(start, size), :]
        at = rank * size
        key_out_ref[at : at + size, :] = block
        if at < half:
            half_ref[at : at + size, :] = block
        if at < quarter:
            quarter_ref[at : at + size, :] = block
    half_ref[half:, :] = ranked_value_ref[:half, :]
    quarter_ref[quarter:, :] = ranked_value_ref[:quarter, :]
    copies[1].wait()
    for start in range(0, width, HD):
        lanes = slice(start, start + HD)
        query = query_ref[:, lanes].astype(jnp.float32)
        query_out_ref[:, lanes] = (query * query_factor * query_gain_ref[:, lanes]).astype(
            jnp.bfloat16
        )


def pack_kernel(parts, *refs):
    sources, (target_ref, sems) = refs[:-2], refs[-2:]
    copies = []
    at = 0
    for place, (source, start, count) in enumerate(parts):
        copies.append(
            pltpu.make_async_copy(
                sources[source].at[pl.ds(start, count), :],
                target_ref.at[pl.ds(at, count), :],
                sems.at[place],
            )
        )
        at += count
    for copy in copies:
        copy.start()
    for copy in copies:
        copy.wait()


def pack(sources, parts):
    width = sources[0].shape[1]
    rows = sum(count for _, _, count in parts)
    anywhere = pl.BlockSpec(memory_space=pl.ANY)
    return pl.pallas_call(
        functools.partial(pack_kernel, parts),
        out_shape=jax.ShapeDtypeStruct((rows, width), jnp.bfloat16),
        in_specs=[anywhere] * len(sources),
        out_specs=anywhere,
        scratch_shapes=[pltpu.SemaphoreType.DMA((len(parts),))],
        compiler_params=pltpu.CompilerParams(vmem_limit_bytes=1 << 20),
        cost_estimate=pl.CostEstimate(flops=0, bytes_accessed=4 * rows * width, transcendentals=0),
    )(*sources)


def attend_kernel(pieces, first, last, operand_count, valid_ref, query_ref, *refs):
    operands = refs[:operand_count]
    rest = refs[operand_count:]
    if not first:
        old_mixed_ref, old_stats_ref = rest[:2]
        rest = rest[2:]
    rows, width = query_ref.shape
    heads = width // HD
    scale = HD ** (-0.5) * LOG2E

    def lanes_of(head):
        return slice(head * HD, (head + 1) * HD)

    def score(head):
        query = query_ref[:, lanes_of(head)]
        return [
            lax.dot_general(
                operands[key_at][start : start + count, lanes_of(head)],
                query,
                (((1,), (1,)), ((), ())),
                preferred_element_type=jnp.float32,
            )
            for key_at, start, _, _, count, _ in pieces
        ]

    def weigh(head, scores):
        tops = []
        for part, (*_, flag) in zip(scores, pieces):
            top = jnp.max(part, axis=0, keepdims=True) * scale
            tops.append(top if flag is None else jnp.where(valid_ref[flag] > 0, top, -FAR))
        top = functools.reduce(jnp.maximum, tops)
        keep = None
        if not first:
            old_top = old_stats_ref[head : head + 1, :]
            top = jnp.maximum(top, old_top)
            keep = jnp.exp2(old_top - top)
        total = None
        weights = []
        for part, (*_, flag) in zip(scores, pieces):
            level = top if flag is None else jnp.where(valid_ref[flag] > 0, top, FAR)
            weight = jnp.exp2(part * scale - level)
            added = jnp.sum(weight, axis=0, keepdims=True)
            total = added if total is None else total + added
            weights.append(weight.astype(jnp.bfloat16))
        weights = weights[0] if len(weights) == 1 else jnp.concatenate(weights, axis=0)
        return top, keep, total, weights

    def mix(head, top, keep, total, weights):
        values = [
            operands[value_at][start : start + count, lanes_of(head)]
            for _, _, value_at, start, count, _ in pieces
        ]
        values = values[0] if len(values) == 1 else jnp.concatenate(values, axis=0)
        mixed = lax.dot_general(
            values, weights, (((0,), (0,)), ((), ())), preferred_element_type=jnp.float32
        )
        if not first:
            mixed = mixed + keep * old_mixed_ref[lanes_of(head), :]
            total = total + keep * old_stats_ref[8 + head : 9 + head, :]
        if last:
            rest[0][:, lanes_of(head)] = (mixed / total).T
        else:
            rest[0][lanes_of(head), :] = mixed
            rest[1][head : head + 1, :] = top
            rest[1][8 + head : 9 + head, :] = total

    scores = score(0)
    waiting = None
    for head in range(heads):
        following = score(head + 1) if head + 1 < heads else None
        weighed = weigh(head, scores)
        if waiting is not None:
            mix(*waiting)
        waiting = (head, *weighed)
        scores = following
    mix(*waiting)


def attend(query, operands, pieces, valid, state=None, last=False):
    rows, width = query.shape
    heads = width // HD
    keys = sum(piece[4] for piece in pieces)
    first = state is None
    mixed = jax.ShapeDtypeStruct((width, rows), jnp.float32)
    stats = jax.ShapeDtypeStruct((16, rows), jnp.float32)
    out = jax.ShapeDtypeStruct((rows, width), jnp.float32)
    inputs = [valid, query, *operands] + ([] if first else list(state))
    vmem = pl.BlockSpec(memory_space=pltpu.VMEM)
    aliases = {}
    if not first and not last:
        aliases = {len(inputs) - 2: 0, len(inputs) - 1: 1}
    moved = 2 * (query.size + sum(operand.size for operand in operands)) + 8 * rows * width
    return pl.pallas_call(
        functools.partial(attend_kernel, pieces, first, last, len(operands)),
        out_shape=out if last else (mixed, stats),
        in_specs=[pl.BlockSpec(memory_space=pltpu.SMEM)] + [vmem] * (len(inputs) - 1),
        out_specs=vmem if last else (vmem, vmem),
        input_output_aliases=aliases,
        compiler_params=pltpu.CompilerParams(vmem_limit_bytes=VMEM_LIMIT),
        cost_estimate=pl.CostEstimate(
            flops=4 * rows * keys * width,
            bytes_accessed=moved,
            transcendentals=rows * keys * heads,
        ),
    )(*inputs)


def on_device(query_proj, key_proj, value_proj, query_gain, key_gain, key_blocks):
    rows, width = query_proj.shape
    width_total = width * lax.axis_size("heads")
    frame_count = lax.axis_size("frames")
    frame = lax.axis_index("frames")
    half, quarter = rows // 2, rows // 4
    smem = pl.BlockSpec(memory_space=pltpu.SMEM)
    vmem = pl.BlockSpec(memory_space=pltpu.VMEM)
    params = pltpu.CompilerParams(vmem_limit_bytes=VMEM_LIMIT)
    block = jax.ShapeDtypeStruct((rows, width), jnp.bfloat16)

    anywhere = pl.BlockSpec(memory_space=pltpu.HBM)
    devices = lax.axis_size("heads")
    own_value, squares = pl.pallas_call(
        gather_kernel,
        out_shape=(block, jax.ShapeDtypeStruct((devices, 2, rows), jnp.float32)),
        in_specs=[anywhere] * 4,
        out_specs=(vmem, vmem),
        scratch_shapes=[pltpu.SMEM(key_blocks.shape, jnp.int32)]
        + [pltpu.VMEM((rows, width), jnp.bfloat16)] * 3
        + [pltpu.SemaphoreType.DMA((4,))],
        compiler_params=params,
        cost_estimate=pl.CostEstimate(flops=4 * rows * width, bytes_accessed=8 * rows * width, transcendentals=0),
    )(
        *(
            pltpu.with_memory_space_constraint(value, pltpu.HBM)
            for value in (key_blocks, query_proj, key_proj, value_proj)
        )
    )
    near_value = [shift(own_value, step) for step in (1, -1)]
    squares = lax.all_to_all(squares, "heads", 0, 0)
    part = lambda count: jax.ShapeDtypeStruct((count, width), jnp.bfloat16)
    query, own_key, own_half, own_quarter = pl.pallas_call(
        functools.partial(norm_kernel, width_total),
        out_shape=(block, block, block, part(half)),
        in_specs=[smem] + [vmem] * 4 + [anywhere] * 2,
        out_specs=(vmem,) * 4,
        scratch_shapes=[pltpu.VMEM((rows, width), jnp.bfloat16)] * 2 + [pltpu.SemaphoreType.DMA((2,))],
        compiler_params=params,
        cost_estimate=pl.CostEstimate(flops=6 * rows * width, bytes_accessed=12 * rows * width, transcendentals=0),
    )(
        key_blocks,
        squares,
        query_gain.reshape(1, width),
        key_gain.reshape(1, width),
        own_value,
        query_proj,
        key_proj,
    )
    distance = jnp.arange(1, 8, dtype=jnp.int32)
    valid = jnp.concatenate([frame - distance >= 0, frame + distance < frame_count]).astype(jnp.int32)

    def flag(side, steps):
        return side * 7 + steps - 1

    both = (1, -1)
    sides = (0, 1)
    near_key = [shift(own_key, step) for step in both]
    state = attend(query, [own_key, own_value], [(0, 0, 1, 0, rows, None)], valid)
    own_half, own_quarter, near_value, state = lax.optimization_barrier(
        (own_half, own_quarter, near_value, state)
    )
    third = [shift(own_half, 3 * step) for step in both]
    fourth = [shift(own_quarter, 4 * step) for step in both]
    *near_key, state = lax.optimization_barrier((*near_key, state))
    relayed = [pack([near_key[side], near_value[side]], [(0, 0, half), (1, 0, half)]) for side in sides]
    second = [shift(value, step) for value, step in zip(relayed, both)]
    passed = [
        pack(
            [near_key[side], near_value[side], third[side]],
            [(0, 0, quarter), (2, 0, quarter), (1, 0, quarter), (2, half, quarter)],
        )
        for side in sides
    ]
    far = [shift(value, 4 * step) for value, step in zip(passed, both)]
    near_key = list(lax.optimization_barrier((*near_key, *relayed, *passed))[:2])
    state = attend(
        query,
        [*near_key, *near_value],
        [(side, 0, 2 + side, 0, rows, flag(side, 1)) for side in sides],
        valid,
        state,
    )
    state = attend(
        query,
        [*third, *fourth],
        [(side, 0, side, half, half, flag(side, 3)) for side in sides]
        + [(2 + side, 0, 2 + side, quarter, quarter, flag(side, 4)) for side in sides],
        valid,
        state,
    )
    *second, state = lax.optimization_barrier((*second, state))
    sixth = [
        shift(pack([second[side]], [(0, 0, quarter), (0, half, quarter)]), 4 * step)
        for side, step in enumerate(both)
    ]
    state = attend(
        query,
        second,
        [(side, 0, side, half, half, flag(side, 2)) for side in sides],
        valid,
        state,
    )
    state = attend(
        query,
        far,
        [
            (side, place * quarter, side, (2 + place) * quarter, quarter, flag(side, steps))
            for side in sides
            for place, steps in enumerate((5, 7))
        ],
        valid,
        state,
    )
    return attend(
        query,
        sixth,
        [(side, 0, side, quarter, quarter, flag(side, 6)) for side in sides],
        valid,
        state,
        last=True,
    )


def solution(mesh):
    placed = (
        P("frames", "heads"),
        P("frames", "heads"),
        P("frames", "heads"),
        P("heads"),
        P("heads"),
        P("frames", None),
    )
    return jax.shard_map(
        on_device, mesh=mesh, in_specs=placed, out_specs=P("frames", "heads"), check_vma=False
    )
```

```python
import functools
import math

import jax
import jax.numpy as jnp
from jax import lax
from jax.experimental import pallas as pl
from jax.experimental.pallas import tpu as pltpu
from jax.sharding import PartitionSpec as P

HD = 128
EPS = 1e-06
LOG2E = math.log2(math.e)
VMEM_LIMIT = 20 << 20
FAR = 1e30


def shift(value, steps):
    count = lax.axis_size("frames")
    initial, last = (max(0, -steps), min(count, count - steps))
    return lax.ppermute(
        value, "frames", [(source, source + steps) for source in range(initial, last)]
    )


def row_squares(value):
    wide = value.astype(jnp.float32)
    wide = wide * wide
    folded = wide[:, :HD]
    for start in range(HD, value.shape[1], HD):
        folded = folded + wide[:, start : start + HD]
    return jnp.sum(folded.T, axis=0, keepdims=True)


def gather_kernel(
    blocks_hbm,
    query_hbm,
    key_hbm,
    value_hbm,
    ranked_ref,
    squares_ref,
    blocks_ref,
    query_ref,
    key_ref,
    value_ref,
    sems,
):
    copies = [
        pltpu.make_async_copy(source, target, sems.at[place])
        for place, (source, target) in enumerate(
            (
                (value_hbm, value_ref),
                (query_hbm, query_ref),
                (key_hbm, key_ref),
                (blocks_hbm, blocks_ref),
            )
        )
    ]
    for copy in copies:
        copy.start()
    copies[3].wait()
    copies[0].wait()
    block_count = blocks_ref.shape[1]
    size = value_ref.shape[0] // block_count
    for rank in range(block_count):
        start = pl.multiple_of(blocks_ref[0, rank] * size, size)
        ranked_ref[rank * size : (rank + 1) * size, :] = value_ref[pl.ds(start, size), :]
    copies[1].wait()
    query_squares = row_squares(query_ref[...])
    copies[2].wait()
    key_squares = row_squares(key_ref[...])
    for device in range(squares_ref.shape[0]):
        squares_ref[device, 0:1, :] = query_squares
        squares_ref[device, 1:2, :] = key_squares


def norm_kernel(
    width_total,
    blocks_ref,
    squares_ref,
    query_gain_ref,
    key_gain_ref,
    ranked_value_ref,
    query_hbm,
    key_hbm,
    query_out_ref,
    key_out_ref,
    half_ref,
    quarter_ref,
    query_ref,
    key_ref,
    sems,
):
    copies = [
        pltpu.make_async_copy(source, target, sems.at[place])
        for place, (source, target) in enumerate(((key_hbm, key_ref), (query_hbm, query_ref)))
    ]
    for copy in copies:
        copy.start()
    rows, width = query_ref.shape
    squares = squares_ref[0]
    for device in range(1, squares_ref.shape[0]):
        squares = squares + squares_ref[device]
    factors = lax.rsqrt(squares / width_total + EPS)
    query_factor = jnp.broadcast_to(factors[0:1, :], (HD, rows)).T
    key_factor = jnp.broadcast_to(factors[1:2, :], (HD, rows)).T
    copies[0].wait()
    for start in range(0, width, HD):
        lanes = slice(start, start + HD)
        key = key_ref[:, lanes].astype(jnp.float32)
        key_ref[:, lanes] = (key * key_factor * key_gain_ref[:, lanes]).astype(jnp.bfloat16)
    block_count = blocks_ref.shape[1]
    size = rows // block_count
    half, quarter = rows // 2, rows // 4
    for rank in range(block_count):
        start = pl.multiple_of(blocks_ref[0, rank] * size, size)
        block = key_ref[pl.ds(start, size), :]
        at = rank * size
        key_out_ref[at : at + size, :] = block
        if at < half:
            half_ref[at : at + size, :] = block
        if at < quarter:
            quarter_ref[at : at + size, :] = block
    half_ref[half:, :] = ranked_value_ref[:half, :]
    quarter_ref[quarter:, :] = ranked_value_ref[:quarter, :]
    copies[1].wait()
    for start in range(0, width, HD):
        lanes = slice(start, start + HD)
        query = query_ref[:, lanes].astype(jnp.float32)
        query_out_ref[:, lanes] = (query * query_factor * query_gain_ref[:, lanes]).astype(
            jnp.bfloat16
        )


def pack_kernel(parts, *refs):
    sources, (target_ref, sems) = refs[:-2], refs[-2:]
    copies = []
    at = 0
    for place, (source, start, count) in enumerate(parts):
        copies.append(
            pltpu.make_async_copy(
                sources[source].at[pl.ds(start, count), :],
                target_ref.at[pl.ds(at, count), :],
                sems.at[place],
            )
        )
        at += count
    for copy in copies:
        copy.start()
    for copy in copies:
        copy.wait()


def pack(sources, parts):
    width = sources[0].shape[1]
    rows = sum(count for _, _, count in parts)
    anywhere = pl.BlockSpec(memory_space=pl.ANY)
    return pl.pallas_call(
        functools.partial(pack_kernel, parts),
        out_shape=jax.ShapeDtypeStruct((rows, width), jnp.bfloat16),
        in_specs=[anywhere] * len(sources),
        out_specs=anywhere,
        scratch_shapes=[pltpu.SemaphoreType.DMA((len(parts),))],
        compiler_params=pltpu.CompilerParams(vmem_limit_bytes=1 << 20),
        cost_estimate=pl.CostEstimate(flops=0, bytes_accessed=4 * rows * width, transcendentals=0),
    )(*sources)


def attend_kernel(pieces, first, last, operand_count, valid_ref, query_ref, *refs):
    operands = refs[:operand_count]
    rest = refs[operand_count:]
    if not first:
        old_mixed_ref, old_stats_ref = rest[:2]
        rest = rest[2:]
    rows, width = query_ref.shape
    heads = width // HD
    scale = HD ** (-0.5) * LOG2E

    def lanes_of(head):
        return slice(head * HD, (head + 1) * HD)

    def score(head):
        query = query_ref[:, lanes_of(head)]
        return [
            lax.dot_general(
                operands[key_at][start : start + count, lanes_of(head)],
                query,
                (((1,), (1,)), ((), ())),
                preferred_element_type=jnp.float32,
            )
            for key_at, start, _, _, count, _ in pieces
        ]

    def weigh(head, scores):
        tops = []
        for part, (*_, flag) in zip(scores, pieces):
            top = jnp.max(part, axis=0, keepdims=True) * scale
            tops.append(top if flag is None else jnp.where(valid_ref[flag] > 0, top, -FAR))
        top = functools.reduce(jnp.maximum, tops)
        keep = None
        if not first:
            old_top = old_stats_ref[head : head + 1, :]
            top = jnp.maximum(top, old_top)
            keep = jnp.exp2(old_top - top)
        total = None
        weights = []
        for part, (*_, flag) in zip(scores, pieces):
            level = top if flag is None else jnp.where(valid_ref[flag] > 0, top, FAR)
            weight = jnp.exp2(part * scale - level)
            added = jnp.sum(weight, axis=0, keepdims=True)
            total = added if total is None else total + added
            weights.append(weight.astype(jnp.bfloat16))
        weights = weights[0] if len(weights) == 1 else jnp.concatenate(weights, axis=0)
        return top, keep, total, weights

    def mix(head, top, keep, total, weights):
        values = [
            operands[value_at][start : start + count, lanes_of(head)]
            for _, _, value_at, start, count, _ in pieces
        ]
        values = values[0] if len(values) == 1 else jnp.concatenate(values, axis=0)
        mixed = lax.dot_general(
            values, weights, (((0,), (0,)), ((), ())), preferred_element_type=jnp.float32
        )
        if not first:
            mixed = mixed + keep * old_mixed_ref[lanes_of(head), :]
            total = total + keep * old_stats_ref[8 + head : 9 + head, :]
        if last:
            rest[0][:, lanes_of(head)] = (mixed / total).T
        else:
            rest[0][lanes_of(head), :] = mixed
            rest[1][head : head + 1, :] = top
            rest[1][8 + head : 9 + head, :] = total

    scores = score(0)
    waiting = None
    for head in range(heads):
        following = score(head + 1) if head + 1 < heads else None
        weighed = weigh(head, scores)
        if waiting is not None:
            mix(*waiting)
        waiting = (head, *weighed)
        scores = following
    mix(*waiting)


def attend(query, operands, pieces, valid, state=None, last=False):
    rows, width = query.shape
    heads = width // HD
    keys = sum(piece[4] for piece in pieces)
    first = state is None
    mixed = jax.ShapeDtypeStruct((width, rows), jnp.float32)
    stats = jax.ShapeDtypeStruct((16, rows), jnp.float32)
    out = jax.ShapeDtypeStruct((rows, width), jnp.float32)
    inputs = [valid, query, *operands] + ([] if first else list(state))
    vmem = pl.BlockSpec(memory_space=pltpu.VMEM)
    aliases = {}
    if not first and not last:
        aliases = {len(inputs) - 2: 0, len(inputs) - 1: 1}
    moved = 2 * (query.size + sum(operand.size for operand in operands)) + 8 * rows * width
    return pl.pallas_call(
        functools.partial(attend_kernel, pieces, first, last, len(operands)),
        out_shape=out if last else (mixed, stats),
        in_specs=[pl.BlockSpec(memory_space=pltpu.SMEM)] + [vmem] * (len(inputs) - 1),
        out_specs=vmem if last else (vmem, vmem),
        input_output_aliases=aliases,
        compiler_params=pltpu.CompilerParams(vmem_limit_bytes=VMEM_LIMIT),
        cost_estimate=pl.CostEstimate(
            flops=4 * rows * keys * width,
            bytes_accessed=moved,
            transcendentals=rows * keys * heads,
        ),
    )(*inputs)


def on_device(query_proj, key_proj, value_proj, query_gain, key_gain, key_blocks):
    rows, width = query_proj.shape
    width_total = width * lax.axis_size("heads")
    frame_count = lax.axis_size("frames")
    frame = lax.axis_index("frames")
    half, quarter = rows // 2, rows // 4
    smem = pl.BlockSpec(memory_space=pltpu.SMEM)
    vmem = pl.BlockSpec(memory_space=pltpu.VMEM)
    params = pltpu.CompilerParams(vmem_limit_bytes=VMEM_LIMIT)
    block = jax.ShapeDtypeStruct((rows, width), jnp.bfloat16)

    anywhere = pl.BlockSpec(memory_space=pltpu.HBM)
    devices = lax.axis_size("heads")
    own_value, squares = pl.pallas_call(
        gather_kernel,
        out_shape=(block, jax.ShapeDtypeStruct((devices, 2, rows), jnp.float32)),
        in_specs=[anywhere] * 4,
        out_specs=(vmem, vmem),
        scratch_shapes=[pltpu.SMEM(key_blocks.shape, jnp.int32)]
        + [pltpu.VMEM((rows, width), jnp.bfloat16)] * 3
        + [pltpu.SemaphoreType.DMA((4,))],
        compiler_params=params,
        cost_estimate=pl.CostEstimate(flops=4 * rows * width, bytes_accessed=8 * rows * width, transcendentals=0),
    )(
        *(
            pltpu.with_memory_space_constraint(value, pltpu.HBM)
            for value in (key_blocks, query_proj, key_proj, value_proj)
        )
    )
    near_value = [shift(own_value, step) for step in (1, -1)]
    squares = lax.all_to_all(squares, "heads", 0, 0)
    part = lambda count: jax.ShapeDtypeStruct((count, width), jnp.bfloat16)
    query, own_key, own_half, own_quarter = pl.pallas_call(
        functools.partial(norm_kernel, width_total),
        out_shape=(block, block, block, part(half)),
        in_specs=[smem] + [vmem] * 4 + [anywhere] * 2,
        out_specs=(vmem,) * 4,
        scratch_shapes=[pltpu.VMEM((rows, width), jnp.bfloat16)] * 2 + [pltpu.SemaphoreType.DMA((2,))],
        compiler_params=params,
        cost_estimate=pl.CostEstimate(flops=6 * rows * width, bytes_accessed=12 * rows * width, transcendentals=0),
    )(
        key_blocks,
        squares,
        query_gain.reshape(1, width),
        key_gain.reshape(1, width),
        own_value,
        query_proj,
        key_proj,
    )
    distance = jnp.arange(1, 8, dtype=jnp.int32)
    valid = jnp.concatenate([frame - distance >= 0, frame + distance < frame_count]).astype(jnp.int32)

    def flag(side, steps):
        return side * 7 + steps - 1

    both = (1, -1)
    sides = (0, 1)
    near_key = [shift(own_key, step) for step in both]
    state = attend(query, [own_key, own_value], [(0, 0, 1, 0, rows, None)], valid)
    own_half, own_quarter, near_value, state = lax.optimization_barrier(
        (own_half, own_quarter, near_value, state)
    )
    third = [shift(own_half, 3 * step) for step in both]
    fourth = [shift(own_quarter, 4 * step) for step in both]
    *near_key, state = lax.optimization_barrier((*near_key, state))
    relayed = [pack([near_key[side], near_value[side]], [(0, 0, half), (1, 0, half)]) for side in sides]
    second = [shift(value, step) for value, step in zip(relayed, both)]
    passed = [
        pack(
            [near_key[side], near_value[side], third[side]],
            [(0, 0, quarter), (2, 0, quarter), (1, 0, quarter), (2, half, quarter)],
        )
        for side in sides
    ]
    far = [shift(value, 4 * step) for value, step in zip(passed, both)]
    near_key = list(lax.optimization_barrier((*near_key, *relayed, *passed))[:2])
    state = attend(
        query,
        [*near_key, *near_value],
        [(side, 0, 2 + side, 0, rows, flag(side, 1)) for side in sides],
        valid,
        state,
    )
    state = attend(
        query,
        [*third, *fourth],
        [(side, 0, side, half, half, flag(side, 3)) for side in sides]
        + [(2 + side, 0, 2 + side, quarter, quarter, flag(side, 4)) for side in sides],
        valid,
        state,
    )
    *second, state = lax.optimization_barrier((*second, state))
    sixth = [
        shift(pack([second[side]], [(0, 0, quarter), (0, half, quarter)]), 4 * step)
        for side, step in enumerate(both)
    ]
    state = attend(
        query,
        second,
        [(side, 0, side, half, half, flag(side, 2)) for side in sides],
        valid,
        state,
    )
    return attend(
        query,
        [*far, *sixth],
        [
            (side, place * quarter, side, (2 + place) * quarter, quarter, flag(side, steps))
            for side in sides
            for place, steps in enumerate((5, 7))
        ]
        + [(2 + side, 0, 2 + side, quarter, quarter, flag(side, 6)) for side in sides],
        valid,
        state,
        last=True,
    )


def solution(mesh):
    placed = (
        P("frames", "heads"),
        P("frames", "heads"),
        P("frames", "heads"),
        P("heads"),
        P("heads"),
        P("frames", None),
    )
    return jax.shard_map(
        on_device, mesh=mesh, in_specs=placed, out_specs=P("frames", "heads"), check_vma=False
    )
```
